32 devices in a mesh: rows: 2 (over core), waves: 16 (over z, y, x).
Axes of the slice: x: 2, y: 2, z: 4, core: 2. Of those that a mesh axis runs over, the one named last changes fastest.
Arguments:
- feats: float32 [8192, 256], P(('rows', 'waves')), may hold values from -6 to 6
- positions: float32 [3, 8192], P(None, ('rows', 'waves')), may hold values from 0 to 6
- cell_counts: int32 [64], P(('rows', 'waves')), may hold values from 1 to 128
- neighbours: int32 [64, 5], P(('rows', 'waves')), may hold values from 0 to 63, as said below
- nbr_count: int32 [64], P(('rows', 'waves')), may hold values from 3 to 5
- kvec: float32 [3, 3072], P(None, 'waves'), may hold values from -4 to 4
- filters: float32 [3072, 256], P('waves'), may hold values from -5 to 5
- w_msg: float32 [256, 256], replicated, may hold values from -0.375 to 0.375
- w_val: float32 [256, 256], replicated, may hold values from -0.375 to 0.375
- w_one: float32 [256, 256], replicated, may hold values from -0.375 to 0.375
- w_two: float32 [256, 256], replicated, may hold values from -0.375 to 0.375
Outputs:
- updated: float32 [8192, 256], P(('rows', 'waves'))
The draws below stay inside these ranges and needn't reach their ends.
Inputs may be any that keep to these rules, and one draw needn't show every extreme that they name: `neighbours`: column 0 of each cell's list is the cell itself, column 1 the cell (c - 2) mod 64, column 2 the cell (c + 2) mod 64; the 5 entries of a list are distinct cells, and every listed cell c' of cell c satisfies (c' - c) mod 64 <= 2 or (c - c') mod 64 <= 2; entries at or beyond nbr_count are in range and unused.
All inputs are finite; a program needn't handle non-finite values.
Results may differ from the reference program's by a relative error of at most 0.0003.
Values sent between devices are 32-bit elements; how exact they have to be, the bound alone decides.
A program may use at most 128 MiB of HBM per device.

```python
import jax
import jax.numpy as jnp
from jax import lax

F = 256
CELL = 128
NB = 5
KWAVES = 3072
CELLS_DEV = 2
CELLS = 64
SLOTS = 8192
DEVICES = 32


def draw_neighbours(key, part):
    span = 2 * CELLS_DEV + 1
    offs = jnp.arange(span, dtype=jnp.int32) - CELLS_DEV
    scores = jax.random.randint(jax.random.fold_in(key, 17), (CELLS, span), 0, 1 << 20)
    scores = scores * span + jnp.arange(span, dtype=jnp.int32)[None, :]
    scores = jnp.where(offs[None, :] == 0, jnp.int32(3 << 28), scores)
    scores = jnp.where(offs[None, :] == -CELLS_DEV, jnp.int32(2 << 28), scores)
    scores = jnp.where(offs[None, :] == CELLS_DEV, jnp.int32(1 << 28), scores)
    order = jnp.argsort(-scores, axis=1, stable=True)[:, :NB]
    chosen = offs[order]
    own = jnp.arange(CELLS, dtype=jnp.int32)[:, None]
    return ((own + chosen) % CELLS).astype(jnp.int32)


def set_ends(entries, rng, low, high):
    longest = entries.shape.index(max(entries.shape))
    spots = []
    for shift in (0, 1):
        where = [jax.random.randint(jax.random.fold_in(rng, axis), (), 0, length) for axis, length in enumerate(entries.shape)]
        where[longest] = (where[longest] + shift) % entries.shape[longest]
        spots.append(tuple(where))
    return entries.at[spots[0]].set(low).at[spots[1]].set(high)


def shard_levels(key, shape, pieces, low, top_value):
    loudness, own = 1.0, jax.random.fold_in(key, 6)
    for dim, blocks in pieces:
        steps = jnp.exp(jax.random.uniform(jax.random.fold_in(own, dim), (blocks,), jnp.float32, low / len(pieces), top_value / len(pieces)))
        loudness = loudness * jnp.repeat(steps, shape[dim] // blocks).reshape([-1 if axis == dim else 1 for axis in range(len(shape))])
    return loudness


def scatter_about(stream_key, shape, deviation, most, split=(), held_as=jnp.bfloat16):
    result = deviation * jax.random.normal(stream_key, shape, jnp.float32)
    if split:
        result = result * shard_levels(stream_key, shape, split, -0.22, 0.18)
    return jnp.clip(result, -most, most).astype(held_as)


def setup_inputs(seed: int = 0) -> dict:
    seeds = jax.random.split(jax.random.key(seed), 12)
    feats = scatter_about(seeds[0], (SLOTS, F), 1.0, 6.0, ((0, 32),), jnp.float32)
    positions = jnp.clip(6.0 * jax.random.uniform(seeds[1], (3, SLOTS), jnp.float32) ** shard_levels(seeds[1], (3, SLOTS), ((1, 32),), -0.2, 0.2), 0.0, 6.0)
    cell_counts = set_ends(jax.random.randint(seeds[2], (CELLS,), 1, CELL + 1), jax.random.fold_in(seeds[2], 1), 1, CELL).astype(jnp.int32)
    neighbours = draw_neighbours(jax.random.fold_in(seeds[11], 71), 0)
    nbr_count = set_ends(jax.random.randint(seeds[4], (CELLS,), 3, NB + 1), jax.random.fold_in(seeds[4], 1), 3, NB).astype(jnp.int32)
    kvec = scatter_about(seeds[5], (3, KWAVES), 1.0, 4.0, ((1, 16),), jnp.float32)
    filters = scatter_about(seeds[6], (KWAVES, F), 1.0, 5.0, ((0, 16),), jnp.float32)
    w_msg = scatter_about(seeds[7], (F, F), F ** -0.5, 0.375, (), jnp.float32)
    w_val = scatter_about(seeds[8], (F, F), F ** -0.5, 0.375, (), jnp.float32)
    w_one = scatter_about(seeds[9], (F, F), F ** -0.5, 0.375, (), jnp.float32)
    w_two = scatter_about(seeds[10], (F, F), F ** -0.5, 0.375, (), jnp.float32)
    return {"feats": feats, "positions": positions, "cell_counts": cell_counts, "neighbours": neighbours, "nbr_count": nbr_count, "kvec": kvec, "filters": filters, "w_msg": w_msg, "w_val": w_val, "w_one": w_one, "w_two": w_two}


HIGH = lax.Precision.HIGHEST

def reference(feats, positions, cell_counts, neighbours, nbr_count, kvec, filters, w_msg, w_val, w_one, w_two):
    slot_ids = jnp.arange(CELL, dtype=jnp.int32)
    valid2 = (slot_ids[None, :] < cell_counts[:, None]).astype(jnp.float32)
    valid = valid2.reshape(-1)
    hw = jnp.dot(feats, w_msg, precision=HIGH)
    vals = jnp.dot(feats, w_val, precision=HIGH) * valid[:, None]
    pos3 = positions.reshape(3, CELLS, CELL)
    hw3 = hw.reshape(CELLS, CELL, F)
    same_slot = jnp.eye(CELL, dtype=jnp.bool_)

    def one_cell(c):
        own = pos3[:, c]
        acc = jnp.zeros((CELL, F), jnp.float32)
        for b in range(NB):
            other = neighbours[c, b]
            near = pos3[:, other]
            dist = lax.optimization_barrier(jnp.sum((own[:, :, None] - near[:, None, :]) ** 2, axis=0))
            live = (b < nbr_count[c]).astype(jnp.float32)
            keep = valid2[c][:, None] * valid2[other][None, :] * live
            weight = jnp.where(same_slot & (other == c), 0.0, jnp.exp(-0.125 * dist) * keep)
            acc = acc + jnp.dot(weight, hw3[other], precision=HIGH)
        return acc
    msg = 0.125 * lax.map(one_cell, jnp.arange(CELLS, dtype=jnp.int32)).reshape(SLOTS, F)
    block = SLOTS // DEVICES
    pos_blocks = positions.reshape(3, DEVICES, block).transpose(1, 0, 2)
    val_blocks = vals.reshape(DEVICES, block, F)

    def forward(carry, item):
        pos_b, val_b = item
        phase = jnp.dot(kvec.T, pos_b, precision=HIGH)
        return ((carry[0] + jnp.dot(jnp.cos(phase), val_b, precision=HIGH), carry[1] + jnp.dot(jnp.sin(phase), val_b, precision=HIGH)), None)
    zero = jnp.zeros((KWAVES, F), jnp.float32)
    (sum_cos, sum_sin), _ = lax.scan(forward, (zero, zero), (pos_blocks, val_blocks))
    filt_cos = filters * sum_cos
    filt_sin = filters * sum_sin

    def backward(pos_b):
        phase = jnp.dot(pos_b.T, kvec, precision=HIGH)
        return jnp.dot(jnp.cos(phase), filt_cos, precision=HIGH) + jnp.dot(jnp.sin(phase), filt_sin, precision=HIGH)
    ewald = lax.map(backward, pos_blocks).reshape(SLOTS, F) / jnp.sqrt(jnp.float32(SLOTS) * jnp.float32(KWAVES))
    total = feats + msg + ewald
    normed = total / jnp.sqrt(lax.optimization_barrier(jnp.mean(total * total, axis=1, keepdims=True)) + 1e-06)
    hidden = jax.nn.silu(jnp.dot(normed, w_one, precision=HIGH))
    return (total + jnp.dot(hidden, w_two, precision=HIGH)) * valid[:, None]
```

```python
import functools
import math

import jax
import jax.numpy as jnp
from jax import lax
from jax.experimental import pallas as pl
from jax.experimental.pallas import tpu as pltpu
from jax.sharding import PartitionSpec as P

MESH = pl.DeviceIdType.MESH
F32 = jnp.float32
BF16 = jnp.bfloat16

SIN = (6.283185302511498, -41.341700405316864, 81.60513138577438, -76.7030153535419, 42.02592698387571, -14.899846661980089, 3.238137503130986)
COS = (0.9999999890590201, -19.739204499453688, 64.93911745988827, -85.45013953077586, 60.16763095018129, -25.96759924584206, 6.528658157862129)


def split(x):
    high = x.astype(BF16)
    return high, (x - high.astype(F32)).astype(BF16)


def mm(a, b):
    return jnp.dot(a, b, preferred_element_type=F32)


def dot3(a, b):
    return mm(a[0], b[0]) + mm(a[0], b[1]) + mm(a[1], b[0])


def sincos(turns):
    x = turns - jnp.floor(turns + 0.5)
    y = x * x
    s = jnp.full_like(y, SIN[-1])
    for coefficient in SIN[-2::-1]:
        s = s * y + coefficient
    c = jnp.full_like(y, COS[-1])
    for coefficient in COS[-2::-1]:
        c = c * y + coefficient
    return s * x, c


def columns(rows):
    height, width = rows.shape
    return jnp.concatenate([rows, jnp.zeros((128 - height, width), F32)], axis=0).T


def body(
    nz, plane, scale,
    counts, neigh, ncount, feats, pos, kv, filt, w_msg, w_val, w_one, w_two,
    out,
    feats_all, pos_all, kv_all, k_cols, ch, cl, sh, sl, fbh, fbl,
    s_acc, xbuf, zs, zr, f_all, fth, ftl, es, er, msg,
    s_pos, r_pos, s_feat, r_feat, s_kv, r_kv, s_x, r_x, s_z, r_z, s_f, r_f, s_g, s_e, r_e,
):
    slots, width = feats.shape
    kb = filt.shape[0]
    half = kb // 2
    kall = nz * kb
    kpad = k_cols.shape[0]
    cells = counts.shape[0]
    cell = slots // cells
    waves = nz * plane
    r = lax.axis_index("rows")
    w = lax.axis_index("waves")
    z = w // plane
    p = w % plane
    other = (1 - r, w)
    at_low = p == 0
    at_high = p == plane - 1
    edge_w = jnp.where(at_low, (w + waves - 1) % waves, (w + 1) % waves)
    crosses = jnp.where(at_low, z == 0, z == nz - 1)
    edge_r = jnp.where(crosses, 1 - r, r)
    edge = (edge_r, edge_w)

    def plane_dev(j):
        return (r, z * plane + (p + j) % plane)

    def z_dev(j):
        return (r, ((z + j) % nz) * plane + p)

    def rcopy(src, dst, ssem, rsem, dev):
        return pltpu.make_async_remote_copy(
            src_ref=src, dst_ref=dst, send_sem=ssem, recv_sem=rsem, device_id=dev, device_id_type=MESH
        )

    def rows_of(block):
        return pl.ds(pl.multiple_of(block * slots, slots), slots)

    barrier = pltpu.get_barrier_semaphore()
    pl.semaphore_signal(barrier, inc=1, device_id=other, device_id_type=MESH)
    for j in range(1, nz):
        pl.semaphore_signal(barrier, inc=1, device_id=z_dev(j), device_id_type=MESH)

    @pl.loop(1, plane)
    def _(j):
        pl.semaphore_signal(barrier, inc=1, device_id=plane_dev(j), device_id_type=MESH)

    @pl.when(at_low | at_high)
    def _():
        pl.semaphore_signal(barrier, inc=1, device_id=edge, device_id_type=MESH)

    pl.semaphore_wait(barrier, nz + plane - 1 + jnp.where(at_low | at_high, 1, 0))

    def kv_copy(j):
        return rcopy(kv, kv_all.at[z], s_kv.at[j], r_kv.at[z], z_dev(j))

    def kv_arrival(j):
        q = (z + j) % nz
        return rcopy(kv, kv_all.at[q], s_kv.at[j], r_kv.at[q], z_dev(j))

    def pos_copy(j):
        return rcopy(pos, pos_all.at[p], s_pos.at[j], r_pos.at[p], plane_dev(j))

    def pos_arrival(q):
        return rcopy(pos, pos_all.at[q], s_pos.at[0], r_pos.at[q], other)

    def feat_copy(j):
        return rcopy(feats, feats_all.at[p], s_feat.at[j], r_feat.at[p], plane_dev(j))

    def feat_arrival(q):
        return rcopy(feats, feats_all.at[q], s_feat.at[0], r_feat.at[q], other)

    edge_pos = rcopy(pos, pos_all.at[plane], s_pos.at[0], r_pos.at[plane], edge)
    edge_feat = rcopy(feats, feats_all.at[plane], s_feat.at[0], r_feat.at[plane], edge)

    for j in range(1, nz):
        kv_copy(j).start()

    @pl.loop(1, plane)
    def _(j):
        pos_copy(j).start()

    @pl.loop(1, plane)
    def _(j):
        feat_copy(j).start()

    @pl.when(at_low | at_high)
    def _():
        edge_pos.start()
        edge_feat.start()

    def place_k(block, rows):
        k_cols[pl.ds(pl.multiple_of(block * kb, 8), kb), :] = columns(rows)[:kb]

    place_k(z, kv[...])
    if kpad > kall:
        k_cols[kall:, :] = jnp.zeros((kpad - kall, 128), F32)
    for j in range(1, nz):
        kv_arrival(j).wait_recv()
        q = (z + j) % nz
        place_k(q, kv_all[q])

    chunk = 32

    def phases(q, rows3):
        px, py, pz = rows3[0:1], rows3[1:2], rows3[2:3]
        lanes = rows_of(q)

        @pl.loop(0, kpad // chunk)
        def _(i):
            ks = pl.ds(pl.multiple_of(i * chunk, chunk), chunk)
            kc = k_cols[ks, :]
            s, c = sincos(kc[:, 0:1] * px + kc[:, 1:2] * py + kc[:, 2:3] * pz)
            a, b = split(c)
            ch[ks, lanes] = a
            cl[ks, lanes] = b
            a, b = split(s)
            sh[ks, lanes] = a
            sl[ks, lanes] = b

    def place_f(q, block):
        a, b = split(block)
        fbh[rows_of(q), :] = a
        fbl[rows_of(q), :] = b

    phases(p, pos[...])
    place_f(p, feats[...])

    @pl.loop(1, plane)
    def _(j):
        q = (p + j) % plane
        pos_arrival(q).wait_recv()
        phases(q, pos_all[q])

    @pl.loop(1, plane)
    def _(j):
        q = (p + j) % plane
        feat_arrival(q).wait_recv()
        place_f(q, feats_all[q])

    natoms = plane * slots

    def partial_sums(zb):
        ks = pl.ds(pl.multiple_of(zb * kb, 8), kb)
        f = (fbh[:natoms, :], fbl[:natoms, :])
        for part, (hi, lo) in enumerate(((ch, cl), (sh, sl))):
            total = dot3((hi[ks, :], lo[ks, :]), f)
            for h in range(2):
                s_acc[zb, h, part] = total[h * half : (h + 1) * half]

    def x_copy(zb):
        return rcopy(s_acc.at[zb, 1 - r], xbuf.at[zb], s_x.at[zb], r_x.at[zb], other)

    def z_copy(j):
        return rcopy(zs.at[j], zr.at[j], s_z.at[j], r_z.at[j], z_dev(j))

    def pass_on(j):
        zb = (z + j) % nz
        x_copy(zb).wait_recv()
        zs[j] = s_acc[zb, r] + xbuf[zb]
        if j:
            z_copy(j).start()

    order = sorted(range(nz), key=lambda j: -min(j, nz - j))
    for i, j in enumerate(order):
        zb = (z + j) % nz
        partial_sums(zb)
        x_copy(zb).start()
        if i:
            pass_on(order[i - 1])
    pass_on(order[-1])

    @pl.when(at_low | at_high)
    def _():
        edge_pos.wait_recv()
        edge_feat.wait_recv()
        place_f(plane, feats_all[plane])

    first = (r * waves + w) * cells
    total_cells = cells * waves * 2
    own_cols = columns(pos[...])
    low_slot = jnp.where(at_low, plane, p - 1)
    high_slot = jnp.where(at_high, plane, p + 1)
    same = lax.broadcasted_iota(jnp.int32, (slots, slots), 0) == lax.broadcasted_iota(
        jnp.int32, (slots, slots), 1
    )
    row_cell = lax.broadcasted_iota(jnp.int32, (slots, slots), 0) // cell
    col_cell = lax.broadcasted_iota(jnp.int32, (slots, slots), 1) // cell

    def listed(c, target):
        found = jnp.float32(0.0)
        for b in range(neigh.shape[1]):
            hit = (neigh[c, b] == target) & (b < ncount[c])
            found = found + jnp.where(hit, 1.0, 0.0)
        return found

    gathered = jnp.zeros((slots, width), F32)
    for shift, slot in ((-1, low_slot), (0, p), (1, high_slot)):
        near = pos[...] if shift == 0 else pos_all[slot]
        dist = jnp.zeros((slots, slots), F32)
        for axis in range(3):
            diff = own_cols[:, axis : axis + 1] - near[axis : axis + 1]
            dist = dist + diff * diff
        live = jnp.zeros((slots, slots), F32)
        for c in range(cells):
            for t in range(cells):
                target = (first + shift * cells + t + total_cells) % total_cells
                live = jnp.where((row_cell == c) & (col_cell == t), listed(c, target), live)
        weight = jnp.exp(-0.125 * dist) * live
        if shift == 0:
            weight = jnp.where(same, 0.0, weight)
        gathered = gathered + dot3(split(weight), (fbh[rows_of(slot), :], fbl[rows_of(slot), :]))
    msg[...] = feats[...] + 0.125 * dot3(split(gathered), split(w_msg[...]))

    total = zs[0]
    for j in range(1, nz):
        z_copy(j).wait_recv()
        total = total + zr[j]
    mine = pl.multiple_of(r * half, 8)
    wv = split(w_val[...])
    own_filter = filt[pl.ds(mine, half), :] * scale

    def share(zb, h):
        return f_all.at[:, pl.ds(pl.multiple_of((zb * 2 + h) * half, 8), half), :]

    for part in range(2):
        f_all[part, pl.ds(pl.multiple_of((z * 2 + r) * half, 8), half), :] = own_filter * dot3(
            split(total[part]), wv
        )
    if kpad > kall:
        f_all[:, kall:, :] = jnp.zeros((2, kpad - kall, width), F32)

    def f_copy(j):
        return rcopy(share(z, r), share(z, r), s_f.at[j], r_f.at[z, r], z_dev(j))

    def f_relay(zb):
        return rcopy(share(zb, r), share(zb, r), s_g.at[zb], r_f.at[zb, r], other)

    def f_arrival(zb, h):
        return rcopy(share(zb, h), share(zb, h), s_g.at[zb], r_f.at[zb, h], other)

    for j in order[:-1]:
        f_copy(j).start()
    f_relay(z).start()
    near_first = order[::-1][1:]
    for j in near_first:
        zb = (z + j) % nz
        f_arrival(zb, r).wait_recv()
        f_relay(zb).start()
    for j in [0] + near_first:
        f_arrival((z + j) % nz, 1 - r).wait_recv()
    for part in range(2):
        a, b = split(f_all[part].T)
        fth[part] = a
        ftl[part] = b

    def back(q):
        lanes = rows_of(q)
        return dot3((fth[0], ftl[0]), (ch[:, lanes], cl[:, lanes])) + dot3(
            (fth[1], ftl[1]), (sh[:, lanes], sl[:, lanes])
        )

    def e_copy(j):
        return rcopy(es.at[j], er.at[j], s_e.at[j], r_e.at[j], plane_dev(j))

    @pl.loop(1, plane)
    def _(j):
        es[j] = back((p + j) % plane)
        e_copy(j).start()

    es[0] = back(p)

    @pl.loop(1, plane)
    def _(j):
        e_copy(j).wait_recv()
        es[0] = es[0] + er[j]

    summed = msg[...] + es[0].T
    normed = summed / jnp.sqrt(jnp.mean(summed * summed, axis=1, keepdims=True) + 1e-06)
    v = dot3(split(normed), split(w_one[...]))
    hidden = v / (1.0 + jnp.exp(-v))
    result = summed + dot3(split(hidden), split(w_two[...]))
    slot_ids = lax.broadcasted_iota(jnp.int32, (cell, width), 0)
    for c in range(cells):
        out[c * cell : (c + 1) * cell, :] = jnp.where(
            slot_ids < counts[c], result[c * cell : (c + 1) * cell], 0.0
        )

    for j in range(1, nz):
        kv_copy(j).wait_send()
        z_copy(j).wait_send()
        f_copy(j).wait_send()
    for zb in range(nz):
        x_copy(zb).wait_send()
        f_relay(zb).wait_send()

    @pl.loop(1, plane)
    def _(j):
        pos_copy(j).wait_send()
        feat_copy(j).wait_send()
        e_copy(j).wait_send()

    @pl.when(at_low | at_high)
    def _():
        edge_pos.wait_send()
        edge_feat.wait_send()


def shards(
    nz, feats, positions, cell_counts, neighbours, nbr_count, kvec, filters, w_msg, w_val, w_one, w_two
):
    cells = cell_counts.shape[0]
    slots, width = feats.shape
    cell = slots // cells
    kb = kvec.shape[1]
    waves = lax.axis_size("waves")
    plane = waves // nz
    devices = lax.axis_size("rows") * waves
    kpad = -(-nz * kb // 128) * 128
    kbpad = -(-kb // 128) * 128
    half = kb // 2
    scale = 1.0 / math.sqrt(float(slots * devices) * float(kb * waves))
    slot_ids = jnp.arange(cell, dtype=jnp.int32)
    valid = (slot_ids[None, :] < cell_counts[:, None]).astype(F32).reshape(-1)
    masked = feats * valid[:, None]
    pos8 = jnp.pad(positions, ((0, 5), (0, 0)))
    kv8 = jnp.pad(kvec * (0.5 / math.pi), ((0, 5), (0, kbpad - kb)))
    natoms = plane * slots
    vm = pltpu.VMEM
    dma = pltpu.SemaphoreType.DMA
    smem_spec = pl.BlockSpec(memory_space=pltpu.SMEM)
    vmem_spec = pl.BlockSpec(memory_space=pltpu.VMEM)
    return pl.pallas_call(
        functools.partial(body, nz, plane, scale),
        out_shape=jax.ShapeDtypeStruct((slots, width), F32),
        in_specs=[smem_spec] * 3 + [vmem_spec] * 8,
        out_specs=vmem_spec,
        scratch_shapes=[
            vm((plane + 1, slots, width), F32),
            vm((plane + 1, 8, slots), F32),
            vm((nz, 8, kbpad), F32),
            vm((kpad, 128), F32),
            vm((kpad, natoms), BF16),
            vm((kpad, natoms), BF16),
            vm((kpad, natoms), BF16),
            vm((kpad, natoms), BF16),
            vm((natoms + slots, width), BF16),
            vm((natoms + slots, width), BF16),
            vm((nz, 2, 2, half, width), F32),
            vm((nz, 2, half, width), F32),
            vm((nz, 2, half, width), F32),
            vm((nz, 2, half, width), F32),
            vm((2, kpad, width), F32),
            vm((2, width, kpad), BF16),
            vm((2, width, kpad), BF16),
            vm((plane, width, slots), F32),
            vm((plane, width, slots), F32),
            vm((slots, width), F32),
            dma((plane,)),
            dma((plane + 1,)),
            dma((plane,)),
            dma((plane + 1,)),
            dma((nz,)),
            dma((nz,)),
            dma((nz,)),
            dma((nz,)),
            dma((nz,)),
            dma((nz,)),
            dma((nz,)),
            dma((nz, 2)),
            dma((nz,)),
            dma((plane,)),
            dma((plane,)),
        ],
        compiler_params=pltpu.CompilerParams(collective_id=0, has_side_effects=True),
        name="ewald_layer",
    )(cell_counts, neighbours, nbr_count, masked, pos8, kv8, filters, w_msg, w_val, w_one, w_two)


def solution(mesh):
    nz = 4 if mesh.shape["waves"] % 4 == 0 else 2
    placed = (
        P(("rows", "waves"), None),
        P(None, ("rows", "waves")),
        P(("rows", "waves")),
        P(("rows", "waves"), None),
        P(("rows", "waves")),
        P(None, "waves"),
        P("waves", None),
        P(),
        P(),
        P(),
        P(),
    )
    return jax.shard_map(
        functools.partial(shards, nz),
        mesh=mesh,
        in_specs=placed,
        out_specs=P(("rows", "waves"), None),
        check_vma=False,
    )
```

```python
import functools
import math

import jax
import jax.numpy as jnp
from jax import lax
from jax.experimental import pallas as pl
from jax.experimental.pallas import tpu as pltpu
from jax.sharding import PartitionSpec as P

MESH = pl.DeviceIdType.MESH
F32 = jnp.float32
BF16 = jnp.bfloat16

SIN = (6.283185302511498, -41.341700405316864, 81.60513138577438, -76.7030153535419, 42.02592698387571, -14.899846661980089, 3.238137503130986)
COS = (0.9999999890590201, -19.739204499453688, 64.93911745988827, -85.45013953077586, 60.16763095018129, -25.96759924584206, 6.528658157862129)


def split(x):
    high = x.astype(BF16)
    return high, (x - high.astype(F32)).astype(BF16)


def mm(a, b):
    return jnp.dot(a, b, preferred_element_type=F32)


def dot3(a, b):
    return mm(a[0], b[0]) + mm(a[0], b[1]) + mm(a[1], b[0])


def sincos(turns):
    x = turns - jnp.floor(turns + 0.5)
    y = x * x
    s = jnp.full_like(y, SIN[-1])
    for coefficient in SIN[-2::-1]:
        s = s * y + coefficient
    c = jnp.full_like(y, COS[-1])
    for coefficient in COS[-2::-1]:
        c = c * y + coefficient
    return s * x, c


def columns(rows):
    height, width = rows.shape
    return jnp.concatenate([rows, jnp.zeros((128 - height, width), F32)], axis=0).T


def body(
    nz, plane, scale,
    counts, neigh, ncount, feats, pos, kv, filt, w_msg, w_val, w_one, w_two,
    out,
    feats_all, pos_all, kv_all, k_cols, ch, cl, sh, sl, fbh, fbl,
    s_acc, xbuf, zs, zr, f_all, fth, ftl, es, er, msg,
    s_pos, r_pos, s_feat, r_feat, s_kv, r_kv, s_x, r_x, s_z, r_z, s_f, r_f, s_g, s_e, r_e,
):
    slots, width = feats.shape
    kb = filt.shape[0]
    half = kb // 2
    kall = nz * kb
    kpad = k_cols.shape[0]
    cells = counts.shape[0]
    cell = slots // cells
    waves = nz * plane
    r = lax.axis_index("rows")
    w = lax.axis_index("waves")
    z = w // plane
    p = w % plane
    other = (1 - r, w)
    at_low = p == 0
    at_high = p == plane - 1
    edge_w = jnp.where(at_low, (w + waves - 1) % waves, (w + 1) % waves)
    crosses = jnp.where(at_low, z == 0, z == nz - 1)
    edge_r = jnp.where(crosses, 1 - r, r)
    edge = (edge_r, edge_w)

    def plane_dev(j):
        return (r, z * plane + (p + j) % plane)

    def z_dev(j):
        return (r, ((z + j) % nz) * plane + p)

    def rcopy(src, dst, ssem, rsem, dev):
        return pltpu.make_async_remote_copy(
            src_ref=src, dst_ref=dst, send_sem=ssem, recv_sem=rsem, device_id=dev, device_id_type=MESH
        )

    def rows_of(block):
        return pl.ds(pl.multiple_of(block * slots, slots), slots)

    barrier = pltpu.get_barrier_semaphore()
    pl.semaphore_signal(barrier, inc=1, device_id=other, device_id_type=MESH)
    for j in range(1, nz):
        pl.semaphore_signal(barrier, inc=1, device_id=z_dev(j), device_id_type=MESH)

    @pl.loop(1, plane)
    def _(j):
        pl.semaphore_signal(barrier, inc=1, device_id=plane_dev(j), device_id_type=MESH)

    @pl.when(at_low | at_high)
    def _():
        pl.semaphore_signal(barrier, inc=1, device_id=edge, device_id_type=MESH)

    pl.semaphore_wait(barrier, nz + plane - 1 + jnp.where(at_low | at_high, 1, 0))

    def kv_copy(j):
        return rcopy(kv, kv_all.at[z], s_kv.at[j], r_kv.at[z], z_dev(j))

    def kv_arrival(j):
        q = (z + j) % nz
        return rcopy(kv, kv_all.at[q], s_kv.at[j], r_kv.at[q], z_dev(j))

    def pos_copy(j):
        return rcopy(pos, pos_all.at[p], s_pos.at[j], r_pos.at[p], plane_dev(j))

    def pos_arrival(q):
        return rcopy(pos, pos_all.at[q], s_pos.at[0], r_pos.at[q], other)

    def feat_copy(j):
        return rcopy(feats, feats_all.at[p], s_feat.at[j], r_feat.at[p], plane_dev(j))

    def feat_arrival(q):
        return rcopy(feats, feats_all.at[q], s_feat.at[0], r_feat.at[q], other)

    edge_pos = rcopy(pos, pos_all.at[plane], s_pos.at[0], r_pos.at[plane], edge)
    edge_feat = rcopy(feats, feats_all.at[plane], s_feat.at[0], r_feat.at[plane], edge)

    for j in range(1, nz):
        kv_copy(j).start()

    @pl.loop(1, plane)
    def _(j):
        pos_copy(j).start()

    @pl.loop(1, plane)
    def _(j):
        feat_copy(j).start()

    @pl.when(at_low | at_high)
    def _():
        edge_pos.start()
        edge_feat.start()

    def place_k(block, rows):
        k_cols[pl.ds(pl.multiple_of(block * kb, 8), kb), :] = columns(rows)[:kb]

    place_k(z, kv[...])
    if kpad > kall:
        k_cols[kall:, :] = jnp.zeros((kpad - kall, 128), F32)
    for j in range(1, nz):
        kv_arrival(j).wait_recv()
        q = (z + j) % nz
        place_k(q, kv_all[q])

    chunk = 32

    def phases(q, rows3):
        px, py, pz = rows3[0:1], rows3[1:2], rows3[2:3]
        lanes = rows_of(q)

        @pl.loop(0, kpad // chunk)
        def _(i):
            ks = pl.ds(pl.multiple_of(i * chunk, chunk), chunk)
            kc = k_cols[ks, :]
            s, c = sincos(kc[:, 0:1] * px + kc[:, 1:2] * py + kc[:, 2:3] * pz)
            a, b = split(c)
            ch[ks, lanes] = a
            cl[ks, lanes] = b
            a, b = split(s)
            sh[ks, lanes] = a
            sl[ks, lanes] = b

    def place_f(q, block):
        a, b = split(block)
        fbh[rows_of(q), :] = a
        fbl[rows_of(q), :] = b

    phases(p, pos[...])
    place_f(p, feats[...])

    @pl.loop(1, plane)
    def _(j):
        q = (p + j) % plane
        pos_arrival(q).wait_recv()
        phases(q, pos_all[q])

    @pl.loop(1, plane)
    def _(j):
        q = (p + j) % plane
        feat_arrival(q).wait_recv()
        place_f(q, feats_all[q])

    natoms = plane * slots

    def partial_sums(zb):
        ks = pl.ds(pl.multiple_of(zb * kb, 8), kb)
        f = (fbh[:natoms, :], fbl[:natoms, :])
        for part, (hi, lo) in enumerate(((ch, cl), (sh, sl))):
            total = dot3((hi[ks, :], lo[ks, :]), f)
            for h in range(2):
                s_acc[zb, h, part] = total[h * half : (h + 1) * half]

    def x_copy(zb):
        return rcopy(s_acc.at[zb, 1 - r], xbuf.at[zb], s_x.at[zb], r_x.at[zb], other)

    def step(up):
        return z_dev(1) if up else z_dev(nz - 1)

    def s_hop(zb, up):
        side = 0 if up else 1
        return rcopy(zs.at[zb], zr.at[side, zb], s_z.at[zb], r_z.at[side, zb], step(up))

    def pass_on(zb):
        x_copy(zb).wait_recv()
        zs[zb] = s_acc[zb, r] + xbuf[zb]
        for up, ahead, behind in ((True, z < zb, z > 0), (False, z > zb, z < nz - 1)):

            @pl.when(ahead & behind)
            def _():
                s_hop(zb, up).wait_recv()
                zs[zb] = zs[zb] + zr[0 if up else 1, zb]

            @pl.when(ahead)
            def _():
                s_hop(zb, up).start()

    order = []
    for i in range(nz // 2):
        order += [nz - 1 - i, i]
    for i, zb in enumerate(order):
        partial_sums(zb)
        x_copy(zb).start()
        if i:
            pass_on(order[i - 1])
    pass_on(order[-1])

    @pl.when(at_low | at_high)
    def _():
        edge_pos.wait_recv()
        edge_feat.wait_recv()
        place_f(plane, feats_all[plane])

    first = (r * waves + w) * cells
    total_cells = cells * waves * 2
    own_cols = columns(pos[...])
    low_slot = jnp.where(at_low, plane, p - 1)
    high_slot = jnp.where(at_high, plane, p + 1)
    same = lax.broadcasted_iota(jnp.int32, (slots, slots), 0) == lax.broadcasted_iota(
        jnp.int32, (slots, slots), 1
    )
    row_cell = lax.broadcasted_iota(jnp.int32, (slots, slots), 0) // cell
    col_cell = lax.broadcasted_iota(jnp.int32, (slots, slots), 1) // cell

    def listed(c, target):
        found = jnp.float32(0.0)
        for b in range(neigh.shape[1]):
            hit = (neigh[c, b] == target) & (b < ncount[c])
            found = found + jnp.where(hit, 1.0, 0.0)
        return found

    gathered = jnp.zeros((slots, width), F32)
    for shift, slot in ((-1, low_slot), (0, p), (1, high_slot)):
        near = pos[...] if shift == 0 else pos_all[slot]
        dist = jnp.zeros((slots, slots), F32)
        for axis in range(3):
            diff = own_cols[:, axis : axis + 1] - near[axis : axis + 1]
            dist = dist + diff * diff
        live = jnp.zeros((slots, slots), F32)
        for c in range(cells):
            for t in range(cells):
                target = (first + shift * cells + t + total_cells) % total_cells
                live = jnp.where((row_cell == c) & (col_cell == t), listed(c, target), live)
        weight = jnp.exp(-0.125 * dist) * live
        if shift == 0:
            weight = jnp.where(same, 0.0, weight)
        gathered = gathered + dot3(split(weight), (fbh[rows_of(slot), :], fbl[rows_of(slot), :]))
    msg[...] = feats[...] + 0.125 * dot3(split(gathered), split(w_msg[...]))

    for up, behind in ((True, z > 0), (False, z < nz - 1)):

        @pl.when(behind)
        def _():
            s_hop(z, up).wait_recv()
            zs[z] = zs[z] + zr[0 if up else 1, z]

    total = zs[z]
    mine = pl.multiple_of(r * half, 8)
    wv = split(w_val[...])
    own_filter = filt[pl.ds(mine, half), :] * scale

    hw = width // 2

    def share(fh, zb, h):
        return f_all.at[fh, :, pl.ds(pl.multiple_of((zb * 2 + h) * half, 8), half), :]

    for part in range(2):
        filtered = own_filter * dot3(split(total[part]), wv)
        for fh in range(2):
            f_all[fh, part, pl.ds(pl.multiple_of((z * 2 + r) * half, 8), half), :] = filtered[
                :, fh * hw : (fh + 1) * hw
            ]
    if kpad > kall:
        f_all[:, :, kall:, :] = jnp.zeros((2, 2, kpad - kall, hw), F32)

    def f_hop(fh, zb, up, d):
        here = share(fh, zb, r)
        return rcopy(here, here, s_f.at[fh, int(up), d], r_f.at[fh, zb, r], step(up))

    def f_relay(fh, zb):
        here = share(fh, zb, r)
        return rcopy(here, here, s_g.at[fh, zb], r_f.at[fh, zb, r], other)

    def f_arrival(fh, zb, h):
        here = share(fh, zb, h)
        return rcopy(here, here, s_g.at[fh, zb], r_f.at[fh, zb, h], other)

    def f_own(fh):
        for up, ahead in ((True, z < nz - 1), (False, z > 0)):

            @pl.when(ahead)
            def _():
                f_hop(fh, z, up, 0).start()

        f_relay(fh, z).start()

    def f_pass(fh, d):
        for up, there, ahead in ((True, z >= d, z < nz - 1), (False, z + d < nz, z > 0)):
            zb = z - d if up else z + d

            @pl.when(there)
            def _():
                f_arrival(fh, zb, r).wait_recv()

            @pl.when(there & ahead)
            def _():
                f_hop(fh, zb, up, d).start()

            @pl.when(there)
            def _():
                f_relay(fh, zb).start()

    def back(fh, q):
        lanes = rows_of(q)
        return dot3((fth[fh, 0], ftl[fh, 0]), (ch[:, lanes], cl[:, lanes])) + dot3(
            (fth[fh, 1], ftl[fh, 1]), (sh[:, lanes], sl[:, lanes])
        )

    def e_copy(fh, j):
        return rcopy(es.at[fh, j], er.at[fh, j], s_e.at[fh, j], r_e.at[fh, j], plane_dev(j))

    def gather_half(fh):
        for zb in range(nz):
            f_arrival(fh, zb, 1 - r).wait_recv()
        for part in range(2):
            a, b = split(f_all[fh, part].T)
            fth[fh, part] = a
            ftl[fh, part] = b

    def back_range(fh, start, stop):
        @pl.loop(start, stop)
        def _(j):
            es[fh, j] = back(fh, (p + j) % plane)
            e_copy(fh, j).start()

    f_own(0)
    for d in range(1, nz):
        f_pass(0, d)
        if d == 1:
            f_own(1)
    gather_half(0)
    cuts = [1 + d * (plane - 1) // (nz - 1) for d in range(nz)]
    for d in range(1, nz):
        f_pass(1, d)
        back_range(0, cuts[d - 1], cuts[d])
    gather_half(1)
    back_range(1, 1, plane)
    for fh in range(2):
        es[fh, 0] = back(fh, p)

    for fh in range(2):

        @pl.loop(1, plane)
        def _(j):
            e_copy(fh, j).wait_recv()
            es[fh, 0] = es[fh, 0] + er[fh, j]

    summed = msg[...] + jnp.concatenate([es[0, 0].T, es[1, 0].T], axis=1)
    normed = summed / jnp.sqrt(jnp.mean(summed * summed, axis=1, keepdims=True) + 1e-06)
    v = dot3(split(normed), split(w_one[...]))
    hidden = v / (1.0 + jnp.exp(-v))
    result = summed + dot3(split(hidden), split(w_two[...]))
    slot_ids = lax.broadcasted_iota(jnp.int32, (cell, width), 0)
    for c in range(cells):
        out[c * cell : (c + 1) * cell, :] = jnp.where(
            slot_ids < counts[c], result[c * cell : (c + 1) * cell], 0.0
        )

    for j in range(1, nz):
        kv_copy(j).wait_send()
    for zb in range(nz):
        x_copy(zb).wait_send()
        for up, ahead in ((True, z < zb), (False, z > zb)):

            @pl.when(ahead)
            def _():
                s_hop(zb, up).wait_send()

        for fh in range(2):
            f_relay(fh, zb).wait_send()
    for fh in range(2):
        for d in range(nz):
            for up, there, ahead in ((True, z >= d, z < nz - 1), (False, z + d < nz, z > 0)):

                @pl.when(there & ahead)
                def _():
                    f_hop(fh, z - d if up else z + d, up, d).wait_send()

    @pl.loop(1, plane)
    def _(j):
        pos_copy(j).wait_send()
        feat_copy(j).wait_send()
        for fh in range(2):
            e_copy(fh, j).wait_send()

    @pl.when(at_low | at_high)
    def _():
        edge_pos.wait_send()
        edge_feat.wait_send()


def shards(
    nz, feats, positions, cell_counts, neighbours, nbr_count, kvec, filters, w_msg, w_val, w_one, w_two
):
    cells = cell_counts.shape[0]
    slots, width = feats.shape
    cell = slots // cells
    kb = kvec.shape[1]
    waves = lax.axis_size("waves")
    plane = waves // nz
    devices = lax.axis_size("rows") * waves
    kpad = -(-nz * kb // 128) * 128
    kbpad = -(-kb // 128) * 128
    half = kb // 2
    scale = 1.0 / math.sqrt(float(slots * devices) * float(kb * waves))
    slot_ids = jnp.arange(cell, dtype=jnp.int32)
    valid = (slot_ids[None, :] < cell_counts[:, None]).astype(F32).reshape(-1)
    masked = feats * valid[:, None]
    pos8 = jnp.pad(positions, ((0, 5), (0, 0)))
    kv8 = jnp.pad(kvec * (0.5 / math.pi), ((0, 5), (0, kbpad - kb)))
    natoms = plane * slots
    vm = pltpu.VMEM
    dma = pltpu.SemaphoreType.DMA
    smem_spec = pl.BlockSpec(memory_space=pltpu.SMEM)
    vmem_spec = pl.BlockSpec(memory_space=pltpu.VMEM)
    return pl.pallas_call(
        functools.partial(body, nz, plane, scale),
        out_shape=jax.ShapeDtypeStruct((slots, width), F32),
        in_specs=[smem_spec] * 3 + [vmem_spec] * 8,
        out_specs=vmem_spec,
        scratch_shapes=[
            vm((plane + 1, slots, width), F32),
            vm((plane + 1, 8, slots), F32),
            vm((nz, 8, kbpad), F32),
            vm((kpad, 128), F32),
            vm((kpad, natoms), BF16),
            vm((kpad, natoms), BF16),
            vm((kpad, natoms), BF16),
            vm((kpad, natoms), BF16),
            vm((natoms + slots, width), BF16),
            vm((natoms + slots, width), BF16),
            vm((nz, 2, 2, half, width), F32),
            vm((nz, 2, half, width), F32),
            vm((nz, 2, half, width), F32),
            vm((2, nz, 2, half, width), F32),
            vm((2, 2, kpad, width // 2), F32),
            vm((2, 2, width // 2, kpad), BF16),
            vm((2, 2, width // 2, kpad), BF16),
            vm((2, plane, width // 2, slots), F32),
            vm((2, plane, width // 2, slots), F32),
            vm((slots, width), F32),
            dma((plane,)),
            dma((plane + 1,)),
            dma((plane,)),
            dma((plane + 1,)),
            dma((nz,)),
            dma((nz,)),
            dma((nz,)),
            dma((nz,)),
            dma((nz,)),
            dma((2, nz)),
            dma((2, 2, nz)),
            dma((2, nz, 2)),
            dma((2, nz)),
            dma((2, plane)),
            dma((2, plane)),
        ],
        compiler_params=pltpu.CompilerParams(collective_id=0, has_side_effects=True),
        name="ewald_layer",
    )(cell_counts, neighbours, nbr_count, masked, pos8, kv8, filters, w_msg, w_val, w_one, w_two)


def solution(mesh):
    nz = 4 if mesh.shape["waves"] % 4 == 0 else 2
    placed = (
        P(("rows", "waves"), None),
        P(None, ("rows", "waves")),
        P(("rows", "waves")),
        P(("rows", "waves"), None),
        P(("rows", "waves")),
        P(None, "waves"),
        P("waves", None),
        P(),
        P(),
        P(),
        P(),
    )
    return jax.shard_map(
        functools.partial(shards, nz),
        mesh=mesh,
        in_specs=placed,
        out_specs=P(("rows", "waves"), None),
        check_vma=False,
    )
```
